128 devices in a mesh: stn: 64 (over x, z, y_lo, core), frq: 2 (over y_hi).
Axes of the slice: x: 4, y: 4 (y_hi: 2, y_lo: 2; y = y_hi * 2 + y_lo), z: 4, core: 2. Of those that a mesh axis runs over, the one named last changes fastest.
Arguments:
- spectra: bfloat16 [512, 2, 8192], P('stn', None, 'frq'), may hold values from -60 to 60, as said below
- pair_bin: int32 [16384, 1], P('stn'), may hold values from 0 to 63; in each aligned block of 256 rows (0 to 255, 256 to 511, ...) at most 10 rows name the same one
- pair_valid: int32 [16384], P('stn'), may hold values 0 or 1
- stack_in: float32 [64, 2048], P('stn', 'frq'), may hold values from -1.5 to 1.5
Outputs:
- stacks: float32 [64, 2048], P('stn', 'frq')
The draws below stay inside these ranges and needn't reach their ends.
Inputs may be any that keep to these rules, and one draw needn't show every extreme that they name: `spectra`: values have rough magnitudes, differing from bin to bin. `pair_bin`: in the 256 rows of one index of stn no bin is named more than 10 times.
All inputs are finite; a program needn't handle non-finite values. No bound on the sum of `pair_valid` on one device may be relied on, other than what follows from the above.
Results may differ from the reference program's by a relative error of at most 0.008.
Values may be sent and summed in bfloat16 or wider, within the bound.
A program may use at most 64 MiB of HBM per device.

```python
import math
import jax
import jax.numpy as jnp
import numpy as np
from jax import lax

STN_DEV = 8
ROUNDS = 4
FREQ = 8192
SAMPLES = 32768
LAGS = 2048
WBLK = 32
STATIONS = 512
PAIRS_DEV = 256
PAIRS = 16384
BINS = 64
CAP = 10
N_STN = 64


def draw_spectra(key, part):
    shape = (STATIONS, 2, FREQ)
    first, second = jax.random.split(key, 2)
    base = jax.random.truncated_normal(first, -6.0, 6.0, shape, jnp.float32)
    factor = jnp.exp(jax.random.uniform(second, shape, jnp.float32, 0.0, math.log(10.0)))
    return (base * factor).astype(jnp.bfloat16)


def set_ends(drawn, stream_key, least, high):
    index_at = [jax.random.randint(jax.random.fold_in(stream_key, axis), (), 0, length) for axis, length in enumerate(drawn.shape)]
    longest = drawn.shape.index(max(drawn.shape))
    beside = index_at[:longest] + [(index_at[longest] + 1) % drawn.shape[longest]] + index_at[longest + 1:]
    return drawn.at[tuple(index_at)].set(least).at[tuple(beside)].set(high)


def steps_of(stream_key, dims, cuts, least, largest):
    gain, own = 1.0, jax.random.fold_in(stream_key, 6)
    for axis_at, blocks in cuts:
        heights = jnp.exp(jax.random.uniform(jax.random.fold_in(own, axis_at), (blocks,), jnp.float32, least / len(cuts), largest / len(cuts)))
        gain = gain * jnp.repeat(heights, dims[axis_at] // blocks).reshape([-1 if axis == axis_at else 1 for axis in range(len(dims))])
    return gain


def routed_block(stream_key, own, number, rows, count, top, reach, slope):
    ranking = jax.random.permutation(stream_key, count)
    crowded, usual = load_shares(count, rows * top, reach, slope, True), load_shares(count, rows * top, reach, slope, False)
    places = jnp.arange(count)

    def named(lengths, turn):
        used = int((lengths > 0).sum())
        fixed = max(1, used // 4)
        shifted = fixed + (places - fixed + turn * (used - fixed)) % max(1, count - fixed)
        return jnp.zeros((count,), jnp.int32).at[ranking[jnp.where(places < fixed, places, shifted)]].set(jnp.asarray(lengths, jnp.int32))

    lengths = jnp.where(number % 4 == 0, named(crowded, number // 4), named(usual, number - number // 4 - 1))
    mixed = jax.random.permutation(jax.random.fold_in(own, 3), count)
    donor, receiver = mixed[0:count // 2 * 2:2], mixed[1:count // 2 * 2:2]
    room = jnp.minimum(lengths[donor] - 1, reach - lengths[receiver]) // 2
    room = jnp.where((donor == ranking[0]) | (receiver == ranking[0]) | (lengths[receiver] == 0), 0, jnp.maximum(room, 0))
    shifted = jax.random.randint(jax.random.fold_in(own, 4), (count // 2,), 0, 1 << 20) % (room + 1)
    lengths = lengths.at[donor].add(-shifted).at[receiver].add(shifted)
    members = jnp.searchsorted(jnp.cumsum(lengths), jnp.arange(rows * top), side="right").astype(jnp.int32)
    grid = members.reshape(top, rows).T
    grid = grid[jax.random.permutation(jax.random.fold_in(own, 1), rows)]
    turn = jax.random.randint(jax.random.fold_in(own, 2), (rows, 1), 0, top)
    return jnp.take_along_axis(grid, (jnp.arange(top)[None, :] + turn) % top, axis=1)


def load_shares(amount, total, limit, lean, full):
    weights = [(1 << 20) // math.isqrt(rank ** lean) + 1 for rank in range(1, amount + 1)]
    largest = limit if full else min(limit, max(-(-total // amount), total * weights[0] // sum(weights)))
    least = 1 if total - largest >= amount - 1 else 0
    holding, surplus = [largest] + [least] * (amount - 1), total - largest - least * (amount - 1)
    while surplus > 0:
        candidates = [i for i in range(1, amount) if holding[i] < largest] or [i for i in range(1, amount) if holding[i] < limit]
        pool, budget = sum([weights[i] for i in candidates]), surplus
        for i in candidates:
            addition = min(limit - holding[i], max(1, budget * weights[i] // pool), surplus)
            holding[i] = holding[i] + addition
            surplus = surplus - addition
    return np.array(holding)


def noise(key, dims, deviation, reach, cuts=(), kind=jnp.bfloat16):
    entries = deviation * jax.random.normal(key, dims, jnp.float32)
    if cuts:
        entries = entries * steps_of(key, dims, cuts, -0.22, 0.18)
    return jnp.clip(entries, -reach, reach).astype(kind)


def setup_inputs(seed: int = 0) -> dict:
    key_list = jax.random.split(jax.random.key(seed), 5)
    spectra = draw_spectra(jax.random.fold_in(key_list[4], 71), 0)
    pair_bin_keys = jax.random.split(jax.random.fold_in(key_list[1], 1), PAIRS // PAIRS_DEV)
    pair_bin_turns = jax.random.permutation(jax.random.fold_in(key_list[1], 3), PAIRS // PAIRS_DEV)
    pair_bin = jax.vmap(lambda own, number: routed_block(jax.random.fold_in(key_list[1], 2), own, number, PAIRS_DEV, BINS, 1, CAP, 2))(pair_bin_keys, pair_bin_turns).reshape((PAIRS, 1))
    pair_valid = set_ends((jax.random.randint(key_list[2], (PAIRS,), 0, 4) < 3).astype(jnp.int32), jax.random.fold_in(key_list[2], 1), 0, 1)
    stack_in = noise(key_list[3], (BINS, LAGS), 0.1, 1.5, ((0, 64), (1, 2)), jnp.float32)
    return {"spectra": spectra, "pair_bin": pair_bin, "pair_valid": pair_valid, "stack_in": stack_in}


def whiten(spectra, count):
    values = spectra.astype(jnp.float32)
    blocks = values.reshape(count, 2, FREQ // WBLK, WBLK)
    power = lax.optimization_barrier(jnp.mean(blocks * blocks, axis=(1, 3), keepdims=True))
    return (blocks / jnp.sqrt(power + 1e-06)).reshape(count, 2, FREQ).astype(jnp.bfloat16)

def cross_block(own, partner):
    own_f = own.astype(jnp.float32)
    part_f = partner.astype(jnp.float32)
    real_part = own_f[:, 0][:, None, :] * part_f[:, 0][None] + own_f[:, 1][:, None, :] * part_f[:, 1][None]
    imag_part = own_f[:, 1][:, None, :] * part_f[:, 0][None] - own_f[:, 0][:, None, :] * part_f[:, 1][None]
    joined = jnp.concatenate([real_part, imag_part], axis=2)
    return joined.reshape(own.shape[0] * partner.shape[0], -1).astype(jnp.bfloat16)

def reference(spectra, pair_bin, pair_valid, stack_in):
    white = whiten(spectra, STATIONS)
    freq_index = 1 + jnp.arange(FREQ, dtype=jnp.int32)
    lag_index = jnp.arange(LAGS, dtype=jnp.int32) - LAGS // 2
    product = freq_index[:, None] * lag_index[None, :] % SAMPLES
    angle = product.astype(jnp.float32) * (2.0 * math.pi / SAMPLES)
    table = jnp.concatenate([jnp.cos(angle), -jnp.sin(angle)], axis=0).astype(jnp.bfloat16)
    grouped = white.reshape(N_STN, STN_DEV, 2, FREQ)
    bin_ids = jnp.arange(BINS, dtype=jnp.int32)

    def per_device(totals, device):
        own = grouped[device]
        pieces = []
        for turn in range(ROUNDS):
            source = ((device - turn - 1) % N_STN).astype(jnp.int32)
            pieces.append(cross_block(own, grouped[source]))
        cross_all = jnp.concatenate(pieces, axis=0)
        corr = jnp.dot(cross_all, table, preferred_element_type=jnp.float32) * (1.0 / FREQ)
        start = (device * PAIRS_DEV).astype(jnp.int32)
        valid = lax.dynamic_slice_in_dim(pair_valid, start, PAIRS_DEV, 0).astype(jnp.float32)
        bins = lax.dynamic_slice_in_dim(pair_bin[:, 0], start, PAIRS_DEV, 0)
        weighted = corr * valid[:, None]
        onehot = (bins[:, None] == bin_ids[None, :]).astype(jnp.float32)
        sums = jnp.dot(onehot.T, weighted, precision=lax.Precision.HIGHEST, preferred_element_type=jnp.float32)
        return (totals + sums, None)
    totals, unused = lax.scan(per_device, jnp.zeros((BINS, LAGS), jnp.float32), jnp.arange(N_STN, dtype=jnp.int32))
    return stack_in + totals
```

```python
import functools
import math

import jax
import jax.numpy as jnp
import numpy as np
from jax import lax
from jax.experimental import pallas as pl
from jax.experimental.pallas import tpu as pltpu
from jax.sharding import PartitionSpec as P

ROUNDS = 4
FREQ = 8192
SAMPLES = 32768
LAGS = 2048
WBLK = 32
STN = 8
BINS = 64
N_STN = 64
N_FRQ = 2
BAND = FREQ // N_FRQ
CHUNK = BAND // N_STN
LANES = 2 * CHUNK
SOURCES = N_STN * N_FRQ
HALF = LAGS // N_FRQ
GROUP = 4
GROUPS = N_STN // GROUP
PERIOD = SAMPLES // CHUNK
PAIRS_DEV = ROUNDS * STN * STN
MESH = pl.DeviceIdType.MESH


def hops(offset):
    return (0, 1, 2, 1)[offset // 4] + (0, 1, 2, 1)[offset % 4]


FAR_FIRST = sorted(range(GROUPS), key=hops, reverse=True)


def tables():
    chunk = np.arange(SOURCES)[:, None] * np.arange(PERIOD)[None, :] % PERIOD
    angle = chunk * (2.0 * math.pi / PERIOD)
    coarse = np.concatenate([np.cos(angle), np.sin(angle)], axis=0).astype(np.float32)
    high = coarse.astype(jnp.bfloat16)
    low = (coarse - high.astype(np.float32)).astype(jnp.bfloat16)
    lag = np.arange(N_FRQ)[:, None, None] * HALF - LAGS // 2 + np.arange(HALF)[None, None, :]
    product = (np.arange(CHUNK)[None, :, None] + 1) * lag % SAMPLES
    turn = product * (2.0 * math.pi / SAMPLES)
    fine = np.concatenate([np.cos(turn), -np.sin(turn)], axis=1) / FREQ
    return high, low, fine.astype(np.float32)


def kernel(
    x_hbm, bin_ref, valid_ref, stack_ref, high_hbm, low_hbm, fine_hbm, out_ref,
    x, send, recv, key_send, keys, first, second, third, fourth, sums, gathered,
    high, low, fine, load_sem, table_sem, send_sem, key_send_sem, recv_sem, key_sem, row_send_sem, row_sem,
):
    me = lax.axis_index("stn")
    band = lax.axis_index("frq")
    my_group = me // GROUP
    my_x, my_z, my_w = me // 16, me // 4 % 4, me % 4

    def peer(offset, turn):
        x_at = (my_x + offset // 4) % 4
        z_at = (my_z + offset % 4) % 4
        return x_at * 16 + z_at * 4 + (my_w + turn) % 4

    load = pltpu.make_async_copy(x_hbm, x, load_sem)
    load.start()
    table_copies = [
        pltpu.make_async_copy(high_hbm, high, table_sem.at[0]),
        pltpu.make_async_copy(low_hbm, low, table_sem.at[1]),
        pltpu.make_async_copy(fine_hbm.at[band], fine, table_sem.at[2]),
    ]

    barrier = pltpu.get_barrier_semaphore()
    for offset in FAR_FIRST:

        def greet(turn, carry, offset=offset):
            pl.semaphore_signal(barrier, inc=1, device_id=(peer(offset, turn), band), device_id_type=MESH)
            return carry

        lax.fori_loop(0 if offset else 1, GROUP, greet, 0)
    pl.semaphore_signal(barrier, inc=1, device_id=(me, 1 - band), device_id_type=MESH)
    for copy in table_copies:
        copy.start()

    lane = lax.broadcasted_iota(jnp.int32, (STN, LANES), 1)
    is_real = lane < CHUNK
    same_block = (
        lax.broadcasted_iota(jnp.int32, (LANES, LANES), 0) // WBLK
        == lax.broadcasted_iota(jnp.int32, (LANES, LANES), 1) // WBLK
    )
    averaging = jnp.where(same_block, 1.0 / (2 * WBLK), 0.0).astype(jnp.bfloat16)

    load.wait()
    wide = 8

    def whiten(step, carry):
        values = []
        for part in range(wide):
            at = pl.multiple_of((step * wide + part) * LANES, LANES)
            both = x[:, :, pl.ds(at, LANES)].astype(jnp.float32)
            values.append((both[:, 0, :], both[:, 1, :]))
        squares = jnp.concatenate([re * re + im * im for re, im in values], axis=0)
        squares_high = squares.astype(jnp.bfloat16)
        squares_low = (squares - squares_high.astype(jnp.float32)).astype(jnp.bfloat16)
        power = jnp.dot(squares_high, averaging, preferred_element_type=jnp.float32) + jnp.dot(
            squares_low, averaging, preferred_element_type=jnp.float32
        )
        scale = lax.rsqrt(power + 1e-06)
        for part, (re, im) in enumerate(values):
            own = scale[part * STN : (part + 1) * STN]
            re, im = re * own, im * own
            even = jnp.where(is_real, re, pltpu.roll(im, CHUNK, 1))
            odd = jnp.where(is_real, pltpu.roll(re, CHUNK, 1), im)
            send[2 * (step * wide + part)] = even.astype(jnp.bfloat16)
            send[2 * (step * wide + part) + 1] = odd.astype(jnp.bfloat16)
        return carry

    lax.fori_loop(0, BAND // LANES // wide, whiten, 0)
    own_key = jnp.where(valid_ref[...] > 0, bin_ref[...], BINS)
    key_send[...] = own_key
    keys[me] = own_key
    recv[me] = send[me]

    pl.semaphore_wait(barrier, N_STN)

    for offset in FAR_FIRST:

        def post(turn, carry, offset=offset):
            to = peer(offset, turn)
            pltpu.make_async_remote_copy(
                src_ref=send.at[to],
                dst_ref=recv.at[me],
                send_sem=send_sem,
                recv_sem=recv_sem.at[my_group],
                device_id=(to, band),
                device_id_type=MESH,
            ).start()
            pltpu.make_async_remote_copy(
                src_ref=key_send,
                dst_ref=keys.at[me],
                send_sem=key_send_sem,
                recv_sem=key_sem.at[my_group],
                device_id=(to, band),
                device_id_type=MESH,
            ).start()
            return carry

        lax.fori_loop(0 if offset else 1, GROUP, post, 0)

    def await_group(group, count):
        some = recv.at[pl.ds(0, count)]
        pltpu.make_async_copy(some, some, recv_sem.at[group]).wait()
        some = keys.at[pl.ds(0, count)]
        pltpu.make_async_copy(some, some, key_sem.at[group]).wait()

    def unpack_group(group):
        for part in range(GROUP):
            block = group * GROUP + part
            white = recv[block].astype(jnp.float32)
            swapped = pltpu.roll(white, CHUNK, 1)
            first[block] = white
            second[block] = swapped
            third[block] = jnp.where(is_real, white, swapped)
            fourth[block] = jnp.where(is_real, swapped, -white)

    bin_row = lax.broadcasted_iota(jnp.int32, (BINS, LANES), 0)

    def bin_group(group):
        total = jnp.zeros((BINS, LANES), jnp.float32)
        for part in range(GROUP):
            block = group * GROUP + part
            partners = [(block + N_STN - turn - 1) % N_STN for turn in range(ROUNDS)]
            straight = [third[partner] for partner in partners]
            crossed = [fourth[partner] for partner in partners]
            pieces = []
            for turn in range(ROUNDS):
                for i in range(STN):
                    own = jnp.broadcast_to(first[block, pl.ds(i, 1), :], (STN, LANES))
                    other = jnp.broadcast_to(second[block, pl.ds(i, 1), :], (STN, LANES))
                    pieces.append(own * straight[turn] + other * crossed[turn])
            cross = jnp.concatenate(pieces, axis=0).astype(jnp.bfloat16)
            onehot = jnp.concatenate(
                [
                    jnp.where(keys[block, pl.ds(row, 1), :] == bin_row, 1.0, 0.0).astype(jnp.bfloat16)
                    for row in range(PAIRS_DEV // LANES)
                ],
                axis=1,
            )
            total += jnp.dot(onehot, cross, preferred_element_type=jnp.float32)
        return total

    await_group(my_group, GROUP - 1)
    unpack_group(my_group)

    def advance(step, total):
        early = step < 9
        side = (step + 1) // 2
        even = step % 2 == 0
        target = jnp.where(early, jnp.where(even, GROUPS - side, side), step - 4)
        needed = jnp.where(early, jnp.where(even, GROUPS - side - 1, side), step - 4)
        needed = (my_group + needed) % GROUPS
        await_group(needed, GROUP)
        unpack_group(needed)
        return total + bin_group((my_group + target) % GROUPS)

    total = lax.fori_loop(0, GROUPS - 1, advance, jnp.zeros((BINS, LANES), jnp.float32))
    total = total + bin_group((my_group + 11) % GROUPS)
    sums[...] = total.reshape(BINS, 1, LANES)
    slot = band * N_STN + me
    gathered[slot] = sums[me]

    for offset in FAR_FIRST:

        def deliver(turn, carry, offset=offset):
            to = peer(offset, turn)
            for there in (1 - band, band):
                pltpu.make_async_remote_copy(
                    src_ref=sums.at[to],
                    dst_ref=gathered.at[slot],
                    send_sem=row_send_sem,
                    recv_sem=row_sem,
                    device_id=(to, there),
                    device_id_type=MESH,
                ).start()
            return carry

        lax.fori_loop(0 if offset else 1, GROUP, deliver, 0)
    pltpu.make_async_remote_copy(
        src_ref=sums.at[me],
        dst_ref=gathered.at[slot],
        send_sem=row_send_sem,
        recv_sem=row_sem,
        device_id=(me, 1 - band),
        device_id_type=MESH,
    ).start()

    for copy in table_copies:
        copy.wait()
    some = send.at[pl.ds(0, N_STN - 1)]
    pltpu.make_async_copy(some, some, send_sem).wait()
    some = keys.at[pl.ds(0, N_STN - 1)]
    pltpu.make_async_copy(some, some, key_send_sem).wait()
    some = gathered.at[pl.ds(0, SOURCES - 1)]
    pltpu.make_async_copy(some, some, row_send_sem).wait()
    pltpu.make_async_copy(some, some, row_sem).wait()

    spectrum = gathered[...].reshape(SOURCES, LANES).T
    turned = jnp.concatenate([-spectrum[CHUNK:], spectrum[:CHUNK]], axis=0)
    left = jnp.concatenate([spectrum, turned], axis=1)
    left_high = left.astype(jnp.bfloat16)
    left_low = (left - left_high.astype(jnp.float32)).astype(jnp.bfloat16)
    mixed = (
        jnp.dot(left_high, high[...], preferred_element_type=jnp.float32)
        + jnp.dot(left_low, high[...], preferred_element_type=jnp.float32)
        + jnp.dot(left_high, low[...], preferred_element_type=jnp.float32)
    )
    for part in range(HALF // PERIOD):
        at = pl.ds(part * PERIOD, PERIOD)
        out_ref[:, at] = stack_ref[:, at] + jnp.sum(mixed * fine[:, at], axis=0, keepdims=True)


def local(spectra, pair_bin, pair_valid, stack_in):
    high, low, fine = tables()
    rows = PAIRS_DEV // LANES
    vmem = pl.BlockSpec(memory_space=pltpu.VMEM)
    anywhere = pl.BlockSpec(memory_space=pl.ANY)
    block = (N_STN, STN, LANES)
    return pl.pallas_call(
        kernel,
        out_shape=jax.ShapeDtypeStruct((1, HALF), jnp.float32),
        in_specs=[anywhere, vmem, vmem, vmem, anywhere, anywhere, anywhere],
        out_specs=vmem,
        scratch_shapes=[
            pltpu.VMEM((STN, 2, BAND), jnp.bfloat16),
            pltpu.VMEM(block, jnp.bfloat16),
            pltpu.VMEM(block, jnp.bfloat16),
            pltpu.VMEM((rows, LANES), jnp.int32),
            pltpu.VMEM((N_STN, rows, LANES), jnp.int32),
            pltpu.VMEM(block, jnp.float32),
            pltpu.VMEM(block, jnp.float32),
            pltpu.VMEM(block, jnp.float32),
            pltpu.VMEM(block, jnp.float32),
            pltpu.VMEM((BINS, 1, LANES), jnp.float32),
            pltpu.VMEM((SOURCES, 1, LANES), jnp.float32),
            pltpu.VMEM(high.shape, jnp.bfloat16),
            pltpu.VMEM(low.shape, jnp.bfloat16),
            pltpu.VMEM(fine.shape[1:], jnp.float32),
            pltpu.SemaphoreType.DMA,
            pltpu.SemaphoreType.DMA((3,)),
            pltpu.SemaphoreType.DMA,
            pltpu.SemaphoreType.DMA,
            pltpu.SemaphoreType.DMA((GROUPS,)),
            pltpu.SemaphoreType.DMA((GROUPS,)),
            pltpu.SemaphoreType.DMA,
            pltpu.SemaphoreType.DMA,
        ],
        compiler_params=pltpu.CompilerParams(
            collective_id=0, has_side_effects=True, vmem_limit_bytes=32 * 2**20
        ),
    )(
        spectra,
        pair_bin.reshape(rows, LANES),
        pair_valid.reshape(rows, LANES),
        stack_in,
        jnp.asarray(high),
        jnp.asarray(low),
        jnp.asarray(fine),
    )


def solution(mesh):
    placed = (P("stn", None, "frq"), P("stn", None), P("stn"), P("stn", "frq"))
    return jax.shard_map(
        local, mesh=mesh, in_specs=placed, out_specs=P("stn", "frq"), check_vma=False
    )
```

```python
import functools
import math

import jax
import jax.numpy as jnp
import numpy as np
from jax import lax
from jax.experimental import pallas as pl
from jax.experimental.pallas import tpu as pltpu
from jax.sharding import PartitionSpec as P

ROUNDS = 4
FREQ = 8192
SAMPLES = 32768
LAGS = 2048
WBLK = 32
STN = 8
BINS = 64
N_STN = 64
N_FRQ = 2
BAND = FREQ // N_FRQ
CHUNK = BAND // N_STN
LANES = 2 * CHUNK
SOURCES = N_STN * N_FRQ
HALF = LAGS // N_FRQ
GROUP = 4
GROUPS = N_STN // GROUP
PERIOD = SAMPLES // CHUNK
PAIRS_DEV = ROUNDS * STN * STN
MESH = pl.DeviceIdType.MESH


def hops(offset):
    return (0, 1, 2, 1)[offset // 4] + (0, 1, 2, 1)[offset % 4]


FAR_FIRST = sorted(range(GROUPS), key=hops, reverse=True)


def tables():
    chunk = np.arange(SOURCES)[:, None] * np.arange(PERIOD)[None, :] % PERIOD
    angle = chunk * (2.0 * math.pi / PERIOD)
    coarse = np.concatenate([np.cos(angle), np.sin(angle)], axis=0).astype(np.float32)
    high = coarse.astype(jnp.bfloat16)
    low = (coarse - high.astype(np.float32)).astype(jnp.bfloat16)
    lag = np.arange(N_FRQ)[:, None, None] * HALF - LAGS // 2 + np.arange(HALF)[None, None, :]
    product = (np.arange(CHUNK)[None, :, None] + 1) * lag % SAMPLES
    turn = product * (2.0 * math.pi / SAMPLES)
    fine = np.concatenate([np.cos(turn), -np.sin(turn)], axis=1) / FREQ
    return high, low, fine.astype(np.float32)


def whiten_own(x, send, accs):
    is_real = lax.broadcasted_iota(jnp.int32, (STN, LANES), 1) < CHUNK
    square = (2 * LANES, 2 * LANES)
    same_block = (
        lax.broadcasted_iota(jnp.int32, square, 0) // WBLK
        == lax.broadcasted_iota(jnp.int32, square, 1) // WBLK
    )
    averaging = jnp.where(same_block, 1.0 / (2 * WBLK), 0.0).astype(jnp.bfloat16)
    for unit in range(len(accs)):
        pltpu.matmul_push_rhs(averaging, 0, unit)
    wide = 8

    def whiten(step, load):
        every = []
        for unit, acc in enumerate(accs):
            values = []
            for part in range(wide):
                at = pl.multiple_of(((step * len(accs) + unit) * wide + part) * LANES, LANES)
                both = x[:, :, pl.ds(at, LANES)].astype(jnp.float32)
                values.append((both[:, 0, :], both[:, 1, :]))
            every.append(values)
            squares = [re * re + im * im for re, im in values]
            squares = jnp.concatenate(
                [jnp.concatenate(squares[: wide // 2], axis=0), jnp.concatenate(squares[wide // 2 :], axis=0)],
                axis=1,
            )
            high = squares.astype(jnp.bfloat16)
            low = (squares - high.astype(jnp.float32)).astype(jnp.bfloat16)
            pltpu.matmul_acc_lhs(acc, high, load)
            pltpu.matmul_acc_lhs(acc, low)
        for unit, acc in enumerate(accs):
            scale = lax.rsqrt(pltpu.matmul_pop(acc) + 1e-06)
            for part, (re, im) in enumerate(every[unit]):
                row, column = part % (wide // 2) * STN, part // (wide // 2) * LANES
                own = scale[row : row + STN, column : column + LANES]
                re, im = re * own, im * own
                even = jnp.where(is_real, re, pltpu.roll(im, CHUNK, 1))
                odd = jnp.where(is_real, pltpu.roll(re, CHUNK, 1), im)
                chunk = 2 * ((step * len(accs) + unit) * wide + part)
                send[chunk] = even.astype(jnp.bfloat16)
                send[chunk + 1] = odd.astype(jnp.bfloat16)

    whiten(0, 0)

    def again(step, carry):
        whiten(step, None)
        return carry

    lax.fori_loop(1, BAND // LANES // wide // len(accs), again, 0)


def binning(recv, keys, first, second, third, fourth, halves):
    is_real = lax.broadcasted_iota(jnp.int32, (STN, LANES), 1) < CHUNK
    bin_row = lax.broadcasted_iota(jnp.int32, (BINS, LANES), 0)

    def twice(one, other):
        return jnp.concatenate([one, other], axis=0).astype(jnp.bfloat16)

    def unpack_group(group):
        for part in range(GROUP):
            block = group * GROUP + part
            white = recv[block].astype(jnp.float32)
            swapped = pltpu.roll(white, CHUNK, 1)
            straight = jnp.where(is_real, white, swapped)
            crossed = jnp.where(is_real, swapped, -white)
            first[block] = white
            second[block] = swapped
            third[block] = twice(straight, straight)
            fourth[block] = twice(crossed, crossed)

    def spread(ref, block, i):
        return twice(
            *(jnp.broadcast_to(ref[block, pl.ds(row, 1), :], (STN, LANES)) for row in (i, i + 1))
        )

    def cross_of(block):
        own = [(spread(first, block, i), spread(second, block, i)) for i in range(0, STN, 2)]
        pieces = []
        for turn in range(ROUNDS):
            partner = (block + N_STN - turn - 1) % N_STN
            straight, crossed = third[partner], fourth[partner]
            pieces += [one * straight + other * crossed for one, other in own]
        return jnp.concatenate(pieces, axis=0)

    def onehot_of(block):
        return jnp.concatenate(
            [
                jnp.where(keys[block, pl.ds(row, 1), :] == bin_row, 1.0, 0.0).astype(jnp.bfloat16)
                for row in range(PAIRS_DEV // LANES)
            ],
            axis=1,
        )

    def bin_group(group):
        for unit, half in enumerate(halves):
            blocks = [group * GROUP + 2 * unit + part for part in range(2)]
            pltpu.matmul_push_rhs(jnp.concatenate([cross_of(block) for block in blocks], axis=1), 0, unit)
            pltpu.matmul_acc_lhs(half, jnp.concatenate([onehot_of(block) for block in blocks], axis=0), 0)

    def binned():
        total = jnp.zeros((BINS, LANES), jnp.float32)
        for half in halves:
            product = pltpu.matmul_pop(half)
            total += product[:BINS, :LANES] + product[BINS:, LANES:]
        return total

    return unpack_group, bin_group, binned


def push_tables(high, low, accs):
    for unit in range(len(accs)):
        at = pl.ds(unit * 2 * LANES, 2 * LANES)
        pltpu.matmul_push_rhs(high[:, at], 0, unit)
        pltpu.matmul_push_rhs(low[:, at], 1, unit)


def transform(gathered, fine, stack_ref, out_ref, accs):
    spectrum = gathered[...].reshape(SOURCES, LANES).T
    turned = jnp.concatenate([-spectrum[CHUNK:], spectrum[:CHUNK]], axis=0)
    left = jnp.concatenate([spectrum, turned], axis=1)
    left_high = left.astype(jnp.bfloat16)
    left_low = (left - left_high.astype(jnp.float32)).astype(jnp.bfloat16)
    for acc in accs:
        pltpu.matmul_acc_lhs(acc, left_high, 0)
        pltpu.matmul_acc_lhs(acc, left_low)
        pltpu.matmul_acc_lhs(acc, left_high, 1)
    for unit, acc in enumerate(accs):
        mixed = pltpu.matmul_pop(acc)
        for part in range(HALF // PERIOD):
            at = pl.ds(part * PERIOD + unit * 2 * LANES, 2 * LANES)
            out_ref[:, at] = stack_ref[:, at] + jnp.sum(mixed * fine[:, at], axis=0, keepdims=True)


def kernel(
    x_hbm, bin_hbm, valid_hbm, stack_hbm, high_hbm, low_hbm, fine_hbm, out_ref,
    x, bin_ref, valid_ref, stack_ref, send, recv, key_send, keys, first, second, third, fourth, sums, gathered,
    high, low, fine, load_sem, table_sem, send_sem, key_send_sem, recv_sem, key_sem, row_send_sem, row_sem,
):
    me = lax.axis_index("stn")
    band = lax.axis_index("frq")
    my_group = me // GROUP
    my_x, my_z, my_w = me // 16, me // 4 % 4, me % 4

    def peer(offset, turn):
        x_at = (my_x + offset // 4) % 4
        z_at = (my_z + offset % 4) % 4
        return x_at * 16 + z_at * 4 + (my_w + turn) % 4

    load = pltpu.make_async_copy(x_hbm, x, load_sem)
    load.start()
    table_copies = [
        pltpu.make_async_copy(high_hbm, high, table_sem.at[0]),
        pltpu.make_async_copy(low_hbm, low, table_sem.at[1]),
        pltpu.make_async_copy(fine_hbm.at[band], fine, table_sem.at[2]),
        pltpu.make_async_copy(stack_hbm, stack_ref, table_sem.at[3]),
    ]
    bin_load = pltpu.make_async_copy(bin_hbm, bin_ref, table_sem.at[4])
    bin_load.start()
    valid_load = pltpu.make_async_copy(valid_hbm, valid_ref, table_sem.at[5])
    valid_load.start()

    barrier = pltpu.get_barrier_semaphore()
    for offset in FAR_FIRST:

        def greet(turn, carry, offset=offset):
            pl.semaphore_signal(barrier, inc=1, device_id=(peer(offset, turn), band), device_id_type=MESH)
            return carry

        lax.fori_loop(0 if offset else 1, GROUP, greet, 0)
    pl.semaphore_signal(barrier, inc=1, device_id=(me, 1 - band), device_id_type=MESH)
    for copy in table_copies:
        copy.start()

    load.wait()
    units = pltpu.ACC(0), pltpu.ACC(1)
    pl.run_scoped(
        lambda *accs: whiten_own(x, send, accs), *(unit((4 * STN, 2 * LANES), jnp.float32) for unit in units)
    )
    bin_load.wait()
    valid_load.wait()
    own_key = jnp.where(valid_ref[...] > 0, bin_ref[...], BINS)
    key_send[...] = own_key
    keys[me] = own_key
    recv[me] = send[me]

    pl.semaphore_wait(barrier, N_STN)

    for offset in FAR_FIRST:

        def post(turn, carry, offset=offset):
            to = peer(offset, turn)
            pltpu.make_async_remote_copy(
                src_ref=send.at[to],
                dst_ref=recv.at[me],
                send_sem=send_sem,
                recv_sem=recv_sem.at[my_group],
                device_id=(to, band),
                device_id_type=MESH,
            ).start()
            pltpu.make_async_remote_copy(
                src_ref=key_send,
                dst_ref=keys.at[me],
                send_sem=key_send_sem,
                recv_sem=key_sem.at[my_group],
                device_id=(to, band),
                device_id_type=MESH,
            ).start()
            return carry

        lax.fori_loop(0 if offset else 1, GROUP, post, 0)

    def await_group(group, count):
        some = recv.at[pl.ds(0, count)]
        pltpu.make_async_copy(some, some, recv_sem.at[group]).wait()
        some = keys.at[pl.ds(0, count)]
        pltpu.make_async_copy(some, some, key_sem.at[group]).wait()

    def plan(step):
        early = step < 9
        side = (step + 1) // 2
        even = step % 2 == 0
        target = jnp.where(early, jnp.where(even, GROUPS - side, side), step - 4)
        needed = jnp.where(early, jnp.where(even, GROUPS - side - 1, side), step - 4)
        return (my_group + target) % GROUPS, (my_group + needed) % GROUPS

    def correlate(*halves):
        unpack_group, bin_group, binned = binning(recv, keys, first, second, third, fourth, halves)
        await_group(my_group, GROUP - 1)
        unpack_group(my_group)
        needed = plan(0)[1]
        await_group(needed, GROUP)
        unpack_group(needed)

        def advance(step, carry):
            target, needed = plan(step - 1)[0], plan(step)[1]
            await_group(needed, GROUP)
            bin_group(target)
            unpack_group(needed)
            return carry

        lax.fori_loop(1, GROUPS - 1, advance, 0)
        bin_group(plan(GROUPS - 2)[0])
        bin_group(plan(GROUPS - 1)[0])
        sums[...] = binned().reshape(BINS, 1, LANES)

    pl.run_scoped(correlate, *(unit((2 * BINS, 2 * LANES), jnp.float32) for unit in units))
    slot = band * N_STN + me
    gathered[slot] = sums[me]

    for offset in FAR_FIRST:

        def deliver(turn, carry, offset=offset):
            to = peer(offset, turn)
            for there in (1 - band, band):
                pltpu.make_async_remote_copy(
                    src_ref=sums.at[to],
                    dst_ref=gathered.at[slot],
                    send_sem=row_send_sem,
                    recv_sem=row_sem,
                    device_id=(to, there),
                    device_id_type=MESH,
                ).start()
            return carry

        lax.fori_loop(0 if offset else 1, GROUP, deliver, 0)
    pltpu.make_async_remote_copy(
        src_ref=sums.at[me],
        dst_ref=gathered.at[slot],
        send_sem=row_send_sem,
        recv_sem=row_sem,
        device_id=(me, 1 - band),
        device_id_type=MESH,
    ).start()

    for copy in table_copies:
        copy.wait()

    def finish(*accs):
        push_tables(high, low, accs)
        some = gathered.at[pl.ds(0, SOURCES - 1)]
        pltpu.make_async_copy(some, some, row_sem).wait()
        transform(gathered, fine, stack_ref, out_ref, accs)

    pl.run_scoped(finish, *(unit((LANES, 2 * LANES), jnp.float32) for unit in units))
    some = send.at[pl.ds(0, N_STN - 1)]
    pltpu.make_async_copy(some, some, send_sem).wait()
    some = keys.at[pl.ds(0, N_STN - 1)]
    pltpu.make_async_copy(some, some, key_send_sem).wait()
    some = gathered.at[pl.ds(0, SOURCES - 1)]
    pltpu.make_async_copy(some, some, row_send_sem).wait()


def local(spectra, pair_bin, pair_valid, stack_in):
    high, low, fine = tables()
    rows = PAIRS_DEV // LANES
    vmem = pl.BlockSpec(memory_space=pltpu.VMEM)
    anywhere = pl.BlockSpec(memory_space=pltpu.HBM)
    block = (N_STN, STN, LANES)
    return pl.pallas_call(
        kernel,
        out_shape=jax.ShapeDtypeStruct((1, HALF), jnp.float32),
        in_specs=[anywhere] * 7,
        out_specs=vmem,
        scratch_shapes=[
            pltpu.VMEM((STN, 2, BAND), jnp.bfloat16),
            pltpu.VMEM((rows, LANES), jnp.int32),
            pltpu.VMEM((rows, LANES), jnp.int32),
            pltpu.VMEM((1, HALF), jnp.float32),
            pltpu.VMEM(block, jnp.bfloat16),
            pltpu.VMEM(block, jnp.bfloat16),
            pltpu.VMEM((rows, LANES), jnp.int32),
            pltpu.VMEM((N_STN, rows, LANES), jnp.int32),
            pltpu.VMEM(block, jnp.float32),
            pltpu.VMEM(block, jnp.float32),
            pltpu.VMEM((N_STN, 2 * STN, LANES), jnp.bfloat16),
            pltpu.VMEM((N_STN, 2 * STN, LANES), jnp.bfloat16),
            pltpu.VMEM((BINS, 1, LANES), jnp.float32),
            pltpu.VMEM((SOURCES, 1, LANES), jnp.float32),
            pltpu.VMEM(high.shape, jnp.bfloat16),
            pltpu.VMEM(low.shape, jnp.bfloat16),
            pltpu.VMEM(fine.shape[1:], jnp.float32),
            pltpu.SemaphoreType.DMA,
            pltpu.SemaphoreType.DMA((6,)),
            pltpu.SemaphoreType.DMA,
            pltpu.SemaphoreType.DMA,
            pltpu.SemaphoreType.DMA((GROUPS,)),
            pltpu.SemaphoreType.DMA((GROUPS,)),
            pltpu.SemaphoreType.DMA,
            pltpu.SemaphoreType.DMA,
        ],
        compiler_params=pltpu.CompilerParams(
            collective_id=0, has_side_effects=True, vmem_limit_bytes=32 * 2**20
        ),
    )(
        *(
            pltpu.with_memory_space_constraint(operand, pltpu.HBM)
            for operand in (
                spectra,
                pair_bin.reshape(rows, LANES),
                pair_valid.reshape(rows, LANES),
                stack_in,
                jnp.asarray(high),
                jnp.asarray(low),
                jnp.asarray(fine),
            )
        )
    )


def solution(mesh):
    placed = (P("stn", None, "frq"), P("stn", None), P("stn"), P("stn", "frq"))
    return jax.shard_map(
        local, mesh=mesh, in_specs=placed, out_specs=P("stn", "frq"), check_vma=False
    )
```

```python
import functools
import math

import jax
import jax.numpy as jnp
import numpy as np
from jax import lax
from jax.experimental import pallas as pl
from jax.experimental.pallas import tpu as pltpu
from jax.sharding import PartitionSpec as P

ROUNDS = 4
FREQ = 8192
SAMPLES = 32768
LAGS = 2048
WBLK = 32
STN = 8
BINS = 64
N_STN = 64
N_FRQ = 2
BAND = FREQ // N_FRQ
LANES = 128
CHUNKS = BAND // LANES
SLOTS = N_FRQ * CHUNKS
HALF = LAGS // N_FRQ
GROUP = 4
GROUPS = N_STN // GROUP
PERIOD = SAMPLES // LANES
PAIRS_DEV = ROUNDS * STN * STN
ROWS = PAIRS_DEV // LANES
FAR_FIRST = (2, 1, 3, 0)
MESH = pl.DeviceIdType.MESH


def tables():
    chunk = np.arange(SLOTS)[:, None] * np.arange(PERIOD)[None, :] % PERIOD
    angle = chunk * (2.0 * math.pi / PERIOD)
    coarse = np.concatenate([np.cos(angle), np.sin(angle)], axis=0).astype(np.float32)
    coarse = np.concatenate([coarse, coarse], axis=0)
    high = coarse.astype(jnp.bfloat16)
    low = (coarse - high.astype(np.float32)).astype(jnp.bfloat16)
    lag = np.arange(N_FRQ)[:, None, None] * HALF - LAGS // 2 + np.arange(HALF)[None, None, :]
    product = (np.arange(LANES)[None, :, None] + 1) * lag % SAMPLES
    turn = product * (2.0 * math.pi / SAMPLES)
    fine = np.concatenate([np.cos(turn), -np.sin(turn)], axis=1) / FREQ
    return high, low, fine.astype(np.float32)


def twice(one, other):
    return jnp.concatenate([one, other], axis=0).astype(jnp.bfloat16)


def whiten_own(x, send, accs):
    square = (2 * LANES, 2 * LANES)
    same_block = (
        lax.broadcasted_iota(jnp.int32, square, 0) // WBLK
        == lax.broadcasted_iota(jnp.int32, square, 1) // WBLK
    )
    averaging = jnp.where(same_block, 1.0 / (2 * WBLK), 0.0).astype(jnp.bfloat16)
    for unit in range(len(accs)):
        pltpu.matmul_push_rhs(averaging, 0, unit)
    wide = 8

    def whiten(step, load):
        every = []
        for unit, acc in enumerate(accs):
            values = []
            for part in range(wide):
                at = pl.multiple_of(((step * len(accs) + unit) * wide + part) * LANES, LANES)
                both = x[:, :, pl.ds(at, LANES)].astype(jnp.float32)
                values.append((both[:, 0, :], both[:, 1, :]))
            every.append(values)
            squares = [re * re + im * im for re, im in values]
            squares = jnp.concatenate(
                [jnp.concatenate(squares[: wide // 2], axis=0), jnp.concatenate(squares[wide // 2 :], axis=0)],
                axis=1,
            )
            high = squares.astype(jnp.bfloat16)
            low = (squares - high.astype(jnp.float32)).astype(jnp.bfloat16)
            pltpu.matmul_acc_lhs(acc, high, load)
            pltpu.matmul_acc_lhs(acc, low)
        for unit, acc in enumerate(accs):
            scale = lax.rsqrt(pltpu.matmul_pop(acc) + 1e-06)
            for part, (re, im) in enumerate(every[unit]):
                row, column = part % (wide // 2) * STN, part // (wide // 2) * LANES
                own = scale[row : row + STN, column : column + LANES]
                send[(step * len(accs) + unit) * wide + part] = twice(re * own, im * own)

    whiten(0, 0)

    def again(step, carry):
        whiten(step, None)
        return carry

    lax.fori_loop(1, CHUNKS // wide // len(accs), again, 0)


def binning(recv, keys, real, imag, reals, imags, halves):
    bin_row = lax.broadcasted_iota(jnp.int32, (BINS, LANES), 0)

    def unpack_group(group):
        for part in range(GROUP):
            block = group * GROUP + part
            white = recv[block].astype(jnp.float32)
            re, im = white[:STN], white[STN:]
            real[block] = re
            imag[block] = im
            reals[block] = twice(re, re)
            imags[block] = twice(im, im)

    def spread(ref, block, i):
        return twice(
            *(jnp.broadcast_to(ref[block, pl.ds(row, 1), :], (STN, LANES)) for row in (i, i + 1))
        )

    def cross_of(block):
        own = [(spread(real, block, i), spread(imag, block, i)) for i in range(0, STN, 2)]
        real_part, imag_part = [], []
        for turn in range(ROUNDS):
            partner = (block + N_STN - turn - 1) % N_STN
            re, im = reals[partner], imags[partner]
            real_part += [one * re + other * im for one, other in own]
            imag_part += [other * re - one * im for one, other in own]
        return jnp.concatenate(
            [jnp.concatenate(real_part, axis=0), jnp.concatenate(imag_part, axis=0)], axis=1
        )

    def onehot_of(block):
        return jnp.concatenate(
            [
                jnp.where(keys[block, pl.ds(row, 1), :] == bin_row, 1.0, 0.0).astype(jnp.bfloat16)
                for row in range(ROWS)
            ],
            axis=1,
        )

    def bin_group(group):
        for part in range(GROUP):
            block = group * GROUP + part
            unit, stage = part % 2, part // 2
            pltpu.matmul_push_rhs(cross_of(block), stage, unit)
            pltpu.matmul_acc_lhs(halves[unit], onehot_of(block), stage)

    def binned():
        return pltpu.matmul_pop(halves[0]) + pltpu.matmul_pop(halves[1])

    return unpack_group, bin_group, binned


def push_tables(high, low, accs):
    for unit in range(len(accs)):
        pltpu.matmul_push_rhs(high[...], 0, unit)
        pltpu.matmul_push_rhs(low[...], 1, unit)


def transform(gathered, fine, stack_ref, out_ref, accs):
    spectrum = gathered[...].reshape(SLOTS, 2 * LANES)
    re, im = spectrum[:, :LANES], spectrum[:, LANES:]
    for acc, upper, lower in zip(accs, (re, im), (-im, re)):
        left = jnp.concatenate([upper, lower], axis=0).T
        left_high = left.astype(jnp.bfloat16)
        left_low = (left - left_high.astype(jnp.float32)).astype(jnp.bfloat16)
        left = jnp.concatenate([left_high, left_low], axis=1)
        pltpu.matmul_acc_lhs(acc, left, 0)
        pltpu.matmul_acc_lhs(acc, left, 1)
    mixed = [pltpu.matmul_pop(acc) for acc in accs]
    for part in range(HALF // PERIOD):
        at = pl.ds(part * PERIOD, PERIOD)
        total = sum(
            jnp.sum(one * fine[pl.ds(unit * LANES, LANES), at], axis=0, keepdims=True)
            for unit, one in enumerate(mixed)
        )
        out_ref[:, at] = stack_ref[:, at] + total


def kernel(
    x_hbm, bin_hbm, valid_hbm, stack_hbm, high_hbm, low_hbm, fine_hbm, out_ref,
    x, bin_ref, valid_ref, stack_ref, send, recv, key_send, keys, real, imag, reals, imags, sums, gathered,
    high, low, fine, load_sem, table_sem, send_sem, key_send_sem, recv_sem, key_sem, row_send_sem, row_sem,
):
    me = lax.axis_index("stn")
    band = lax.axis_index("frq")
    my_group = me // GROUP
    my_x, my_z, my_w = me // 16, me // 4 % 4, me % 4
    gathers = my_z < 2
    my_chunk = my_x * 8 + my_z * 4 + my_w
    units = pltpu.ACC(0), pltpu.ACC(1)

    load = pltpu.make_async_copy(x_hbm, x, load_sem)
    load.start()
    table_copies = [
        pltpu.make_async_copy(high_hbm, high, table_sem.at[0]),
        pltpu.make_async_copy(low_hbm, low, table_sem.at[1]),
        pltpu.make_async_copy(fine_hbm.at[band], fine, table_sem.at[2]),
        pltpu.make_async_copy(stack_hbm, stack_ref, table_sem.at[3]),
    ]
    bin_load = pltpu.make_async_copy(bin_hbm, bin_ref, table_sem.at[4])
    bin_load.start()
    valid_load = pltpu.make_async_copy(valid_hbm, valid_ref, table_sem.at[5])
    valid_load.start()

    barrier = pltpu.get_barrier_semaphore()
    pl.semaphore_signal(barrier, inc=1, device_id=(me, 1 - band), device_id_type=MESH)

    @pl.when(gathers)
    def _():
        for x_off in FAR_FIRST:

            def greet(step, carry, x_off=x_off):
                to = (my_x + x_off) % 4 * 16 + (my_z + 2 + step // 4) % 4 * 4 + (my_w + step) % 4
                pl.semaphore_signal(barrier, inc=1, device_id=(to, band), device_id_type=MESH)
                return carry

            lax.fori_loop(0, 16 if x_off else 8, greet, 0)
        for z_off in (1, 0):

            def greet_near(step, carry, z_off=z_off):
                to = my_x * 16 + (my_z + z_off) % 4 * 4 + (my_w + step) % 4
                pl.semaphore_signal(barrier, inc=1, device_id=(to, band), device_id_type=MESH)
                return carry

            lax.fori_loop(0 if z_off else 1, GROUP, greet_near, 0)

    for copy in table_copies:
        copy.start()
    load.wait()
    pl.run_scoped(
        lambda *accs: whiten_own(x, send, accs), *(unit((4 * STN, 2 * LANES), jnp.float32) for unit in units)
    )
    bin_load.wait()
    valid_load.wait()
    own_key = jnp.where(valid_ref[...] > 0, bin_ref[...], BINS)
    key_send[...] = own_key

    @pl.when(gathers)
    def _():
        keys[me] = own_key
        recv[me] = send[my_chunk]
        pl.semaphore_wait(barrier, CHUNKS)

    @pl.when(jnp.logical_not(gathers))
    def _():
        pl.semaphore_wait(barrier, CHUNKS + 1)

    for x_off in FAR_FIRST:

        def post(step, carry, x_off=x_off):
            to_x, to_z, to_w = (my_x + x_off) % 4, step // 4, (my_w + step) % 4
            to = to_x * 16 + to_z * 4 + to_w

            def start():
                pltpu.make_async_remote_copy(
                    src_ref=send.at[to_x * 8 + to_z * 4 + to_w],
                    dst_ref=recv.at[me],
                    send_sem=send_sem,
                    recv_sem=recv_sem.at[my_group],
                    device_id=(to, band),
                    device_id_type=MESH,
                ).start()
                pltpu.make_async_remote_copy(
                    src_ref=key_send,
                    dst_ref=keys.at[me],
                    send_sem=key_send_sem,
                    recv_sem=key_sem.at[my_group],
                    device_id=(to, band),
                    device_id_type=MESH,
                ).start()

            if x_off:
                start()
            else:
                pl.when(to != me)(start)
            return carry

        lax.fori_loop(0, 8, post, 0)

    def await_all(ref, count, sem):
        some = ref.at[pl.ds(0, count)]
        pltpu.make_async_copy(some, some, sem).wait()

    def await_group(group, count):
        await_all(recv, count, recv_sem.at[group])
        await_all(keys, count, key_sem.at[group])

    def plan(step):
        early = step < 9
        side = (step + 1) // 2
        even = step % 2 == 0
        target = jnp.where(early, jnp.where(even, GROUPS - side, side), step - 4)
        needed = jnp.where(early, jnp.where(even, GROUPS - side - 1, side), step - 4)
        return (my_group + target) % GROUPS, (my_group + needed) % GROUPS

    def correlate(*halves):
        unpack_group, bin_group, binned = binning(recv, keys, real, imag, reals, imags, halves)
        await_group(my_group, GROUP - 1)
        unpack_group(my_group)
        needed = plan(0)[1]
        await_group(needed, GROUP)
        unpack_group(needed)

        def advance(step, carry):
            target, needed = plan(step - 1)[0], plan(step)[1]
            await_group(needed, GROUP)
            bin_group(target)
            unpack_group(needed)
            return carry

        lax.fori_loop(1, GROUPS - 1, advance, 0)
        bin_group(plan(GROUPS - 2)[0])
        bin_group(plan(GROUPS - 1)[0])
        sums[...] = binned().reshape(BINS, 1, 2 * LANES)

    slot = band * CHUNKS + my_chunk

    @pl.when(gathers)
    def _():
        pl.run_scoped(correlate, *(unit((BINS, 2 * LANES), jnp.float32) for unit in units))
        gathered[slot] = sums[me]

        def deliver(step, carry):
            to = step // 8 % 4 * 16 + step // 32 * 4 + step % 4
            there = step // 4 % 2

            @pl.when(jnp.logical_or(to != me, there != band))
            def _():
                pltpu.make_async_remote_copy(
                    src_ref=sums.at[to],
                    dst_ref=gathered.at[slot],
                    send_sem=row_send_sem,
                    recv_sem=row_sem,
                    device_id=(to, there),
                    device_id_type=MESH,
                ).start()

            return carry

        lax.fori_loop(0, N_STN * N_FRQ, deliver, 0)

    for copy in table_copies:
        copy.wait()

    def finish(*accs):
        push_tables(high, low, accs)

        @pl.when(gathers)
        def _():
            await_all(gathered, SLOTS - 1, row_sem)

        @pl.when(jnp.logical_not(gathers))
        def _():
            await_all(gathered, SLOTS, row_sem)

        transform(gathered, fine, stack_ref, out_ref, accs)

    pl.run_scoped(finish, *(unit((LANES, 2 * LANES), jnp.float32) for unit in units))

    @pl.when(gathers)
    def _():
        await_all(send, CHUNKS - 1, send_sem)
        await_all(keys, CHUNKS - 1, key_send_sem)
        await_all(gathered, SLOTS - 1, row_send_sem)
        await_all(gathered, SLOTS, row_send_sem)

    @pl.when(jnp.logical_not(gathers))
    def _():
        await_all(send, CHUNKS, send_sem)
        await_all(keys, CHUNKS, key_send_sem)


def local(spectra, pair_bin, pair_valid, stack_in):
    high, low, fine = tables()
    block = (N_STN, STN, LANES)
    twin = (N_STN, 2 * STN, LANES)
    return pl.pallas_call(
        kernel,
        out_shape=jax.ShapeDtypeStruct((1, HALF), jnp.float32),
        in_specs=[pl.BlockSpec(memory_space=pltpu.HBM)] * 7,
        out_specs=pl.BlockSpec(memory_space=pltpu.VMEM),
        scratch_shapes=[
            pltpu.VMEM((STN, 2, BAND), jnp.bfloat16),
            pltpu.VMEM((ROWS, LANES), jnp.int32),
            pltpu.VMEM((ROWS, LANES), jnp.int32),
            pltpu.VMEM((1, HALF), jnp.float32),
            pltpu.VMEM((CHUNKS, 2 * STN, LANES), jnp.bfloat16),
            pltpu.VMEM(twin, jnp.bfloat16),
            pltpu.VMEM((ROWS, LANES), jnp.int32),
            pltpu.VMEM((N_STN, ROWS, LANES), jnp.int32),
            pltpu.VMEM(block, jnp.float32),
            pltpu.VMEM(block, jnp.float32),
            pltpu.VMEM(twin, jnp.bfloat16),
            pltpu.VMEM(twin, jnp.bfloat16),
            pltpu.VMEM((BINS, 1, 2 * LANES), jnp.float32),
            pltpu.VMEM((SLOTS, 1, 2 * LANES), jnp.float32),
            pltpu.VMEM(high.shape, jnp.bfloat16),
            pltpu.VMEM(low.shape, jnp.bfloat16),
            pltpu.VMEM(fine.shape[1:], jnp.float32),
            pltpu.SemaphoreType.DMA,
            pltpu.SemaphoreType.DMA((6,)),
            pltpu.SemaphoreType.DMA,
            pltpu.SemaphoreType.DMA,
            pltpu.SemaphoreType.DMA((GROUPS,)),
            pltpu.SemaphoreType.DMA((GROUPS,)),
            pltpu.SemaphoreType.DMA,
            pltpu.SemaphoreType.DMA,
        ],
        compiler_params=pltpu.CompilerParams(
            collective_id=0, has_side_effects=True, vmem_limit_bytes=32 * 2**20
        ),
    )(
        *(
            pltpu.with_memory_space_constraint(operand, pltpu.HBM)
            for operand in (
                spectra,
                pair_bin.reshape(ROWS, LANES),
                pair_valid.reshape(ROWS, LANES),
                stack_in,
                jnp.asarray(high),
                jnp.asarray(low),
                jnp.asarray(fine),
            )
        )
    )


def solution(mesh):
    placed = (P("stn", None, "frq"), P("stn", None), P("stn"), P("stn", "frq"))
    return jax.shard_map(
        local, mesh=mesh, in_specs=placed, out_specs=P("stn", "frq"), check_vma=False
    )
```

```python
import functools
import math

import jax
import jax.numpy as jnp
import numpy as np
from jax import lax
from jax.experimental import pallas as pl
from jax.experimental.pallas import tpu as pltpu
from jax.sharding import PartitionSpec as P

ROUNDS = 4
FREQ = 8192
SAMPLES = 32768
LAGS = 2048
WBLK = 32
STN = 8
BINS = 64
N_STN = 64
N_FRQ = 2
BAND = FREQ // N_FRQ
LANES = 128
CHUNKS = BAND // LANES
SLOTS = N_FRQ * CHUNKS
HALF = LAGS // N_FRQ
GROUP = 4
GROUPS = N_STN // GROUP
PERIOD = SAMPLES // LANES
PAIRS_DEV = ROUNDS * STN * STN
ROWS = PAIRS_DEV // LANES
FAR_FIRST = (0, 1, 3, 2)
MESH = pl.DeviceIdType.MESH


def tables():
    chunk = np.arange(SLOTS)[:, None] * np.arange(PERIOD)[None, :] % PERIOD
    angle = chunk * (2.0 * math.pi / PERIOD)
    coarse = np.concatenate([np.cos(angle), np.sin(angle)], axis=0).astype(np.float32)
    coarse = np.concatenate([coarse, coarse], axis=0)
    high = coarse.astype(jnp.bfloat16)
    low = (coarse - high.astype(np.float32)).astype(jnp.bfloat16)
    lag = np.arange(N_FRQ)[:, None, None] * HALF - LAGS // 2 + np.arange(HALF)[None, None, :]
    product = (np.arange(LANES)[None, :, None] + 1) * lag % SAMPLES
    turn = product * (2.0 * math.pi / SAMPLES)
    fine = np.concatenate([np.cos(turn), -np.sin(turn)], axis=1) / FREQ
    return high, low, fine.astype(np.float32)


def twice(one, other):
    return jnp.concatenate([one, other], axis=0).astype(jnp.bfloat16)


def whiten_own(x, send, accs):
    square = (2 * LANES, 2 * LANES)
    same_block = (
        lax.broadcasted_iota(jnp.int32, square, 0) // WBLK
        == lax.broadcasted_iota(jnp.int32, square, 1) // WBLK
    )
    averaging = jnp.where(same_block, 1.0 / (2 * WBLK), 0.0).astype(jnp.bfloat16)
    for unit in range(len(accs)):
        pltpu.matmul_push_rhs(averaging, 0, unit)
    wide = 8

    def whiten(step, load):
        every = []
        for unit, acc in enumerate(accs):
            values = []
            for part in range(wide):
                at = pl.multiple_of(((step * len(accs) + unit) * wide + part) * LANES, LANES)
                both = x[:, :, pl.ds(at, LANES)].astype(jnp.float32)
                values.append((both[:, 0, :], both[:, 1, :]))
            every.append(values)
            squares = [re * re + im * im for re, im in values]
            squares = jnp.concatenate(
                [jnp.concatenate(squares[: wide // 2], axis=0), jnp.concatenate(squares[wide // 2 :], axis=0)],
                axis=1,
            )
            high = squares.astype(jnp.bfloat16)
            low = (squares - high.astype(jnp.float32)).astype(jnp.bfloat16)
            pltpu.matmul_acc_lhs(acc, high, load)
            pltpu.matmul_acc_lhs(acc, low)
        for unit, acc in enumerate(accs):
            scale = lax.rsqrt(pltpu.matmul_pop(acc) + 1e-06)
            for part, (re, im) in enumerate(every[unit]):
                row, column = part % (wide // 2) * STN, part // (wide // 2) * LANES
                own = scale[row : row + STN, column : column + LANES]
                send[(step * len(accs) + unit) * wide + part] = twice(re * own, im * own)

    whiten(0, 0)

    def again(step, carry):
        whiten(step, None)
        return carry

    lax.fori_loop(1, CHUNKS // wide // len(accs), again, 0)


def binning(recv, keys, wide_keys, real, imag, reals, imags, halves):
    bin_row = lax.broadcasted_iota(jnp.int32, (BINS, LANES), 0).astype(jnp.float32)

    def unpack_group(group):
        for part in range(GROUP):
            block = group * GROUP + part
            white = recv[block].astype(jnp.float32)
            re, im = white[:STN], white[STN:]
            wide_keys[block] = keys[block].astype(jnp.float32)
            real[block] = re
            imag[block] = im
            reals[block] = twice(re, re)
            imags[block] = twice(im, im)

    def spread(ref, block, i):
        return twice(
            *(jnp.broadcast_to(ref[block, pl.ds(row, 1), :], (STN, LANES)) for row in (i, i + 1))
        )

    def cross_of(block):
        own = [(spread(real, block, i), spread(imag, block, i)) for i in range(0, STN, 2)]
        real_part, imag_part = [], []
        for turn in range(ROUNDS):
            partner = (block + N_STN - turn - 1) % N_STN
            re, im = reals[partner], imags[partner]
            real_part += [one * re + other * im for one, other in own]
            imag_part += [other * re - one * im for one, other in own]
        return jnp.concatenate(
            [jnp.concatenate(real_part, axis=0), jnp.concatenate(imag_part, axis=0)], axis=1
        )

    def onehot_of(block):
        return jnp.concatenate(
            [
                jnp.where(wide_keys[block, pl.ds(row, 1), :] == bin_row, 1.0, 0.0).astype(jnp.bfloat16)
                for row in range(ROWS)
            ],
            axis=1,
        )

    def bin_group(group):
        for part in range(GROUP):
            block = group * GROUP + part
            unit, stage = part % 2, part // 2
            pltpu.matmul_push_rhs(cross_of(block), stage, unit)
            pltpu.matmul_acc_lhs(halves[unit], onehot_of(block), stage)

    def binned():
        return pltpu.matmul_pop(halves[0]) + pltpu.matmul_pop(halves[1])

    return unpack_group, bin_group, binned


def push_tables(high, low, accs):
    for unit in range(len(accs)):
        pltpu.matmul_push_rhs(high[...], 0, unit)
        pltpu.matmul_push_rhs(low[...], 1, unit)


def transform(gathered, fine, stack_ref, out_ref, accs):
    spectrum = gathered[...].reshape(SLOTS, 2 * LANES)
    re, im = spectrum[:, :LANES], spectrum[:, LANES:]
    for acc, upper, lower in zip(accs, (re, im), (-im, re)):
        left = jnp.concatenate([upper, lower], axis=0).T
        left_high = left.astype(jnp.bfloat16)
        left_low = (left - left_high.astype(jnp.float32)).astype(jnp.bfloat16)
        left = jnp.concatenate([left_high, left_low], axis=1)
        pltpu.matmul_acc_lhs(acc, left, 0)
        pltpu.matmul_acc_lhs(acc, left, 1)
    mixed = [pltpu.matmul_pop(acc) for acc in accs]
    for part in range(HALF // PERIOD):
        at = pl.ds(part * PERIOD, PERIOD)
        total = sum(
            jnp.sum(one * fine[pl.ds(unit * LANES, LANES), at], axis=0, keepdims=True)
            for unit, one in enumerate(mixed)
        )
        out_ref[:, at] = stack_ref[:, at] + total


def kernel(
    x_hbm, bin_hbm, valid_hbm, stack_hbm, high_hbm, low_hbm, fine_hbm, out_ref,
    x, bin_ref, valid_ref, stack_ref, send, recv, key_send, keys, wide_keys, real, imag, reals, imags, sums, gathered,
    high, low, fine, load_sem, table_sem, send_sem, key_send_sem, recv_sem, key_sem, row_send_sem, row_sem,
):
    me = lax.axis_index("stn")
    band = lax.axis_index("frq")
    my_group = me // GROUP
    my_x, my_z, my_w = me // 16, me // 4 % 4, me % 4
    gathers = my_z < 2
    my_chunk = my_x * 8 + my_z * 4 + my_w
    units = pltpu.ACC(0), pltpu.ACC(1)

    barrier = pltpu.get_barrier_semaphore()
    pl.semaphore_signal(barrier, inc=1, device_id=(me, 1 - band), device_id_type=MESH)

    @pl.when(gathers)
    def _():
        for x_off in (2, 1, 3, 0):

            def greet(step, carry, x_off=x_off):
                to = (my_x + x_off) % 4 * 16 + (my_z + 2 + step // 4) % 4 * 4 + (my_w + step) % 4
                pl.semaphore_signal(barrier, inc=1, device_id=(to, band), device_id_type=MESH)
                return carry

            lax.fori_loop(0, 16 if x_off else 8, greet, 0, unroll=True)
        for z_off in (1, 0):

            def greet_near(step, carry, z_off=z_off):
                to = my_x * 16 + (my_z + z_off) % 4 * 4 + (my_w + step) % 4
                pl.semaphore_signal(barrier, inc=1, device_id=(to, band), device_id_type=MESH)
                return carry

            lax.fori_loop(0 if z_off else 1, GROUP, greet_near, 0)

    load = pltpu.make_async_copy(x_hbm, x, load_sem)
    load.start()
    table_copies = [
        pltpu.make_async_copy(high_hbm, high, table_sem.at[0]),
        pltpu.make_async_copy(low_hbm, low, table_sem.at[1]),
        pltpu.make_async_copy(fine_hbm.at[band], fine, table_sem.at[2]),
        pltpu.make_async_copy(stack_hbm, stack_ref, table_sem.at[3]),
    ]
    bin_load = pltpu.make_async_copy(bin_hbm, bin_ref, table_sem.at[4])
    bin_load.start()
    valid_load = pltpu.make_async_copy(valid_hbm, valid_ref, table_sem.at[5])
    valid_load.start()

    for copy in table_copies:
        copy.start()
    load.wait()
    pl.run_scoped(
        lambda *accs: whiten_own(x, send, accs), *(unit((4 * STN, 2 * LANES), jnp.float32) for unit in units)
    )
    bin_load.wait()
    valid_load.wait()
    own_key = jnp.where(valid_ref[...] > 0, bin_ref[...], BINS).astype(jnp.float32).astype(jnp.bfloat16)
    key_send[...] = own_key

    @pl.when(gathers)
    def _():
        keys[me] = own_key
        recv[me] = send[my_chunk]
        pl.semaphore_wait(barrier, CHUNKS)

    @pl.when(jnp.logical_not(gathers))
    def _():
        pl.semaphore_wait(barrier, CHUNKS + 1)

    for x_off in FAR_FIRST:

        def post(step, carry, x_off=x_off):
            to_x, to_z, to_w = (my_x + x_off) % 4, step // 4, (my_w + step) % 4
            to = to_x * 16 + to_z * 4 + to_w

            def start():
                pltpu.make_async_remote_copy(
                    src_ref=send.at[to_x * 8 + to_z * 4 + to_w],
                    dst_ref=recv.at[me],
                    send_sem=send_sem,
                    recv_sem=recv_sem.at[my_group],
                    device_id=(to, band),
                    device_id_type=MESH,
                ).start()
                pltpu.make_async_remote_copy(
                    src_ref=key_send,
                    dst_ref=keys.at[me],
                    send_sem=key_send_sem,
                    recv_sem=key_sem.at[my_group],
                    device_id=(to, band),
                    device_id_type=MESH,
                ).start()

            if x_off:
                start()
            else:
                pl.when(to != me)(start)
            return carry

        lax.fori_loop(0, 8, post, 0, unroll=True)

    def await_all(ref, count, sem):
        some = ref.at[pl.ds(0, count)]
        pltpu.make_async_copy(some, some, sem).wait()

    def await_group(group, count):
        await_all(recv, count, recv_sem.at[group])
        await_all(keys, count, key_sem.at[group])

    def plan(step):
        early = step < 9
        side = (step + 1) // 2
        even = step % 2 == 0
        target = jnp.where(early, jnp.where(even, GROUPS - side, side), step - 4)
        needed = jnp.where(early, jnp.where(even, GROUPS - side - 1, side), step - 4)
        return (my_group + target) % GROUPS, (my_group + needed) % GROUPS

    def correlate(*halves):
        unpack_group, bin_group, binned = binning(recv, keys, wide_keys, real, imag, reals, imags, halves)
        await_group(my_group, GROUP - 1)
        unpack_group(my_group)
        needed = plan(0)[1]
        await_group(needed, GROUP)
        unpack_group(needed)

        def advance(step, carry):
            target, needed = plan(step - 1)[0], plan(step)[1]
            await_group(needed, GROUP)
            bin_group(target)
            unpack_group(needed)
            return carry

        lax.fori_loop(1, GROUPS - 1, advance, 0)
        bin_group(plan(GROUPS - 2)[0])
        bin_group(plan(GROUPS - 1)[0])
        sums[...] = binned().reshape(BINS, 1, 2 * LANES)

    slot = band * CHUNKS + my_chunk

    @pl.when(gathers)
    def _():
        pl.run_scoped(correlate, *(unit((BINS, 2 * LANES), jnp.float32) for unit in units))
        gathered[slot] = sums[me]

        for there in range(N_FRQ):
            for y_low in range(2):
                for z_at in range(4):
                    base = z_at * 4 + y_low * 2

                    def deliver(step, carry, base=base, there=there):
                        to = step // 2 * 16 + base + step % 2

                        @pl.when(jnp.logical_or(to != me, there != band))
                        def _():
                            pltpu.make_async_remote_copy(
                                src_ref=sums.at[to],
                                dst_ref=gathered.at[slot],
                                send_sem=row_send_sem,
                                recv_sem=row_sem,
                                device_id=(to, there),
                                device_id_type=MESH,
                            ).start()

                        return carry

                    lax.fori_loop(0, 8, deliver, 0, unroll=True)

    for copy in table_copies:
        copy.wait()

    def finish(*accs):
        push_tables(high, low, accs)

        @pl.when(gathers)
        def _():
            await_all(gathered, SLOTS - 1, row_sem)

        @pl.when(jnp.logical_not(gathers))
        def _():
            await_all(gathered, SLOTS, row_sem)

        transform(gathered, fine, stack_ref, out_ref, accs)

    pl.run_scoped(finish, *(unit((LANES, 2 * LANES), jnp.float32) for unit in units))

    @pl.when(gathers)
    def _():
        await_all(send, CHUNKS - 1, send_sem)
        await_all(keys, CHUNKS - 1, key_send_sem)
        await_all(gathered, SLOTS - 1, row_send_sem)
        await_all(gathered, SLOTS, row_send_sem)

    @pl.when(jnp.logical_not(gathers))
    def _():
        await_all(send, CHUNKS, send_sem)
        await_all(keys, CHUNKS, key_send_sem)


def local(spectra, pair_bin, pair_valid, stack_in):
    high, low, fine = tables()
    block = (N_STN, STN, LANES)
    twin = (N_STN, 2 * STN, LANES)
    return pl.pallas_call(
        kernel,
        out_shape=jax.ShapeDtypeStruct((1, HALF), jnp.float32),
        in_specs=[pl.BlockSpec(memory_space=pltpu.HBM)] * 7,
        out_specs=pl.BlockSpec(memory_space=pltpu.VMEM),
        scratch_shapes=[
            pltpu.VMEM((STN, 2, BAND), jnp.bfloat16),
            pltpu.VMEM((ROWS, LANES), jnp.int32),
            pltpu.VMEM((ROWS, LANES), jnp.int32),
            pltpu.VMEM((1, HALF), jnp.float32),
            pltpu.VMEM((CHUNKS, 2 * STN, LANES), jnp.bfloat16),
            pltpu.VMEM(twin, jnp.bfloat16),
            pltpu.VMEM((ROWS, LANES), jnp.bfloat16),
            pltpu.VMEM((N_STN, ROWS, LANES), jnp.bfloat16),
            pltpu.VMEM((N_STN, ROWS, LANES), jnp.float32),
            pltpu.VMEM(block, jnp.float32),
            pltpu.VMEM(block, jnp.float32),
            pltpu.VMEM(twin, jnp.bfloat16),
            pltpu.VMEM(twin, jnp.bfloat16),
            pltpu.VMEM((BINS, 1, 2 * LANES), jnp.float32),
            pltpu.VMEM((SLOTS, 1, 2 * LANES), jnp.float32),
            pltpu.VMEM(high.shape, jnp.bfloat16),
            pltpu.VMEM(low.shape, jnp.bfloat16),
            pltpu.VMEM(fine.shape[1:], jnp.float32),
            pltpu.SemaphoreType.DMA,
            pltpu.SemaphoreType.DMA((6,)),
            pltpu.SemaphoreType.DMA,
            pltpu.SemaphoreType.DMA,
            pltpu.SemaphoreType.DMA((GROUPS,)),
            pltpu.SemaphoreType.DMA((GROUPS,)),
            pltpu.SemaphoreType.DMA,
            pltpu.SemaphoreType.DMA,
        ],
        compiler_params=pltpu.CompilerParams(
            collective_id=0, has_side_effects=True, vmem_limit_bytes=32 * 2**20
        ),
    )(
        *(
            pltpu.with_memory_space_constraint(operand, pltpu.HBM)
            for operand in (
                spectra,
                pair_bin.reshape(ROWS, LANES),
                pair_valid.reshape(ROWS, LANES),
                stack_in,
                jnp.asarray(high),
                jnp.asarray(low),
                jnp.asarray(fine),
            )
        )
    )


def solution(mesh):
    placed = (P("stn", None, "frq"), P("stn", None), P("stn"), P("stn", "frq"))
    return jax.shard_map(
        local, mesh=mesh, in_specs=placed, out_specs=P("stn", "frq"), check_vma=False
    )
```

```python
import functools
import math

import jax
import jax.numpy as jnp
import numpy as np
from jax import lax
from jax.experimental import pallas as pl
from jax.experimental.pallas import tpu as pltpu
from jax.sharding import PartitionSpec as P

ROUNDS = 4
FREQ = 8192
SAMPLES = 32768
LAGS = 2048
WBLK = 32
STN = 8
BINS = 64
N_STN = 64
N_FRQ = 2
BAND = FREQ // N_FRQ
LANES = 128
CHUNKS = BAND // LANES
SLOTS = N_FRQ * CHUNKS
HALF = LAGS // N_FRQ
GROUP = 4
GROUPS = N_STN // GROUP
PERIOD = SAMPLES // LANES
PAIRS_DEV = ROUNDS * STN * STN
ROWS = PAIRS_DEV // LANES
FAR_FIRST = (0, 1, 3, 2)
MESH = pl.DeviceIdType.MESH


def tables():
    chunk = np.arange(SLOTS)[:, None] * np.arange(PERIOD)[None, :] % PERIOD
    angle = chunk * (2.0 * math.pi / PERIOD)
    coarse = np.concatenate([np.cos(angle), np.sin(angle)], axis=0).astype(np.float32)
    coarse = np.concatenate([coarse, coarse], axis=0)
    high = coarse.astype(jnp.bfloat16)
    low = (coarse - high.astype(np.float32)).astype(jnp.bfloat16)
    lag = np.arange(N_FRQ)[:, None, None] * HALF - LAGS // 2 + np.arange(HALF)[None, None, :]
    product = (np.arange(LANES)[None, :, None] + 1) * lag % SAMPLES
    turn = product * (2.0 * math.pi / SAMPLES)
    fine = np.concatenate([np.cos(turn), -np.sin(turn)], axis=1) / FREQ
    return high, low, fine.astype(np.float32)


def twice(one, other):
    return jnp.concatenate([one, other], axis=0).astype(jnp.bfloat16)


def whiten_own(x, send, accs):
    square = (2 * LANES, 2 * LANES)
    same_block = (
        lax.broadcasted_iota(jnp.int32, square, 0) // WBLK
        == lax.broadcasted_iota(jnp.int32, square, 1) // WBLK
    )
    averaging = jnp.where(same_block, 1.0 / (2 * WBLK), 0.0).astype(jnp.bfloat16)
    for unit in range(len(accs)):
        pltpu.matmul_push_rhs(averaging, 0, unit)
    wide = 8

    def whiten(step, load):
        every = []
        for unit, acc in enumerate(accs):
            values = []
            for part in range(wide):
                at = pl.multiple_of(((step * len(accs) + unit) * wide + part) * LANES, LANES)
                both = x[:, :, pl.ds(at, LANES)].astype(jnp.float32)
                values.append((both[:, 0, :], both[:, 1, :]))
            every.append(values)
            squares = [re * re + im * im for re, im in values]
            squares = jnp.concatenate(
                [jnp.concatenate(squares[: wide // 2], axis=0), jnp.concatenate(squares[wide // 2 :], axis=0)],
                axis=1,
            )
            high = squares.astype(jnp.bfloat16)
            low = (squares - high.astype(jnp.float32)).astype(jnp.bfloat16)
            pltpu.matmul_acc_lhs(acc, high, load)
            pltpu.matmul_acc_lhs(acc, low)
        for unit, acc in enumerate(accs):
            scale = lax.rsqrt(pltpu.matmul_pop(acc) + 1e-06)
            for part, (re, im) in enumerate(every[unit]):
                row, column = part % (wide // 2) * STN, part // (wide // 2) * LANES
                own = scale[row : row + STN, column : column + LANES]
                send[(step * len(accs) + unit) * wide + part] = twice(re * own, im * own)

    whiten(0, 0)

    def again(step, carry):
        whiten(step, None)
        return carry

    lax.fori_loop(1, CHUNKS // wide // len(accs), again, 0)


def binning(recv, keys, wide_keys, real, imag, reals, imags, halves):
    bin_row = lax.broadcasted_iota(jnp.int32, (BINS, LANES), 0).astype(jnp.float32)

    def unpack_group(group):
        for part in range(GROUP):
            block = group * GROUP + part
            white = recv[block].astype(jnp.float32)
            re, im = white[:STN], white[STN:]
            wide_keys[block] = keys[block].astype(jnp.float32)
            real[block] = re
            imag[block] = im
            reals[block] = twice(re, re)
            imags[block] = twice(im, im)

    def spread(ref, block, i):
        return twice(
            *(jnp.broadcast_to(ref[block, pl.ds(row, 1), :], (STN, LANES)) for row in (i, i + 1))
        )

    def cross_of(block):
        own = [(spread(real, block, i), spread(imag, block, i)) for i in range(0, STN, 2)]
        real_part, imag_part = [], []
        for turn in range(ROUNDS):
            partner = (block + N_STN - turn - 1) % N_STN
            re, im = reals[partner], imags[partner]
            real_part += [one * re + other * im for one, other in own]
            imag_part += [other * re - one * im for one, other in own]
        return jnp.concatenate(
            [jnp.concatenate(real_part, axis=0), jnp.concatenate(imag_part, axis=0)], axis=1
        )

    def onehot_of(block):
        return jnp.concatenate(
            [
                jnp.where(wide_keys[block, pl.ds(row, 1), :] == bin_row, 1.0, 0.0).astype(jnp.bfloat16)
                for row in range(ROWS)
            ],
            axis=1,
        )

    def bin_group(group):
        for part in range(GROUP):
            block = group * GROUP + part
            unit, stage = part % 2, part // 2
            pltpu.matmul_push_rhs(cross_of(block), stage, unit)
            pltpu.matmul_acc_lhs(halves[unit], onehot_of(block), stage)

    def binned():
        return pltpu.matmul_pop(halves[0]) + pltpu.matmul_pop(halves[1])

    return unpack_group, bin_group, binned


def push_tables(high, low, accs):
    for unit in range(len(accs)):
        pltpu.matmul_push_rhs(high[...], 0, unit)
        pltpu.matmul_push_rhs(low[...], 1, unit)


def transform(gathered, fine, stack_ref, out_ref, accs):
    spectrum = gathered[...].reshape(SLOTS, 2 * LANES)
    re, im = spectrum[:, :LANES], spectrum[:, LANES:]
    for acc, upper, lower in zip(accs, (re, im), (-im, re)):
        left = jnp.concatenate([upper, lower], axis=0).T
        left_high = left.astype(jnp.bfloat16)
        left_low = (left - left_high.astype(jnp.float32)).astype(jnp.bfloat16)
        left = jnp.concatenate([left_high, left_low], axis=1)
        pltpu.matmul_acc_lhs(acc, left, 0)
        pltpu.matmul_acc_lhs(acc, left, 1)
    mixed = [pltpu.matmul_pop(acc) for acc in accs]
    for part in range(HALF // PERIOD):
        at = pl.ds(part * PERIOD, PERIOD)
        products = [one * fine[pl.ds(unit * LANES, LANES), at] for unit, one in enumerate(mixed)]
        total = jnp.sum(products[0] + products[1], axis=0, keepdims=True)
        out_ref[:, at] = stack_ref[:, at] + total


def kernel(
    x_hbm, bin_hbm, valid_hbm, stack_hbm, high_hbm, low_hbm, fine_hbm, out_ref,
    x, bin_ref, valid_ref, stack_ref, send, recv, key_send, keys, wide_keys, real, imag, reals, imags, sums, gathered,
    high, low, fine, load_sem, table_sem, send_sem, key_send_sem, recv_sem, key_sem, row_send_sem, row_sem,
):
    me = lax.axis_index("stn")
    band = lax.axis_index("frq")
    my_group = me // GROUP
    my_x, my_z, my_w = me // 16, me // 4 % 4, me % 4
    gathers = my_z < 2
    my_chunk = my_x * 8 + my_z * 4 + my_w
    units = pltpu.ACC(0), pltpu.ACC(1)

    barrier = pltpu.get_barrier_semaphore()
    pl.semaphore_signal(barrier, inc=1, device_id=(me, 1 - band), device_id_type=MESH)

    @pl.when(gathers)
    def _():
        for x_off in (2, 1, 3, 0):

            def greet(step, carry, x_off=x_off):
                to = (my_x + x_off) % 4 * 16 + (my_z + 2 + step // 4) % 4 * 4 + (my_w + step) % 4
                pl.semaphore_signal(barrier, inc=1, device_id=(to, band), device_id_type=MESH)
                return carry

            lax.fori_loop(0, 16 if x_off else 8, greet, 0, unroll=True)
        for z_off in (1, 0):

            def greet_near(step, carry, z_off=z_off):
                to = my_x * 16 + (my_z + z_off) % 4 * 4 + (my_w + step) % 4
                pl.semaphore_signal(barrier, inc=1, device_id=(to, band), device_id_type=MESH)
                return carry

            lax.fori_loop(0 if z_off else 1, GROUP, greet_near, 0, unroll=True)

    load = pltpu.make_async_copy(x_hbm, x, load_sem)
    load.start()
    table_copies = [
        pltpu.make_async_copy(high_hbm, high, table_sem.at[0]),
        pltpu.make_async_copy(low_hbm, low, table_sem.at[1]),
        pltpu.make_async_copy(fine_hbm.at[band], fine, table_sem.at[2]),
        pltpu.make_async_copy(stack_hbm, stack_ref, table_sem.at[3]),
    ]
    bin_load = pltpu.make_async_copy(bin_hbm, bin_ref, table_sem.at[4])
    bin_load.start()
    valid_load = pltpu.make_async_copy(valid_hbm, valid_ref, table_sem.at[5])
    valid_load.start()

    for copy in table_copies:
        copy.start()
    load.wait()
    pl.run_scoped(
        lambda *accs: whiten_own(x, send, accs), *(unit((4 * STN, 2 * LANES), jnp.float32) for unit in units)
    )
    bin_load.wait()
    valid_load.wait()
    own_key = jnp.where(valid_ref[...] > 0, bin_ref[...], BINS).astype(jnp.float32).astype(jnp.bfloat16)
    key_send[...] = own_key

    @pl.when(gathers)
    def _():
        keys[me] = own_key
        recv[me] = send[my_chunk]
        pl.semaphore_wait(barrier, CHUNKS)

    @pl.when(jnp.logical_not(gathers))
    def _():
        pl.semaphore_wait(barrier, CHUNKS + 1)

    for x_off in FAR_FIRST:

        def post(step, carry, x_off=x_off):
            to_x, to_z, to_w = (my_x + x_off) % 4, step // 4, (my_w + step) % 4
            to = to_x * 16 + to_z * 4 + to_w

            def start():
                pltpu.make_async_remote_copy(
                    src_ref=send.at[to_x * 8 + to_z * 4 + to_w],
                    dst_ref=recv.at[me],
                    send_sem=send_sem,
                    recv_sem=recv_sem.at[my_group],
                    device_id=(to, band),
                    device_id_type=MESH,
                ).start()
                pltpu.make_async_remote_copy(
                    src_ref=key_send,
                    dst_ref=keys.at[me],
                    send_sem=key_send_sem,
                    recv_sem=key_sem.at[my_group],
                    device_id=(to, band),
                    device_id_type=MESH,
                ).start()

            if x_off:
                start()
            else:
                pl.when(to != me)(start)
            return carry

        lax.fori_loop(0, 8, post, 0, unroll=True)

    def await_all(ref, count, sem):
        some = ref.at[pl.ds(0, count)]
        pltpu.make_async_copy(some, some, sem).wait()

    def await_group(group, count):
        await_all(recv, count, recv_sem.at[group])
        await_all(keys, count, key_sem.at[group])

    def plan(step):
        early = step < 9
        side = (step + 1) // 2
        even = step % 2 == 0
        target = jnp.where(early, jnp.where(even, GROUPS - side, side), step - 4)
        needed = jnp.where(early, jnp.where(even, GROUPS - side - 1, side), step - 4)
        return (my_group + target) % GROUPS, (my_group + needed) % GROUPS

    def correlate(*halves):
        unpack_group, bin_group, binned = binning(recv, keys, wide_keys, real, imag, reals, imags, halves)
        await_group(my_group, GROUP - 1)
        unpack_group(my_group)
        needed = plan(0)[1]
        await_group(needed, GROUP)
        unpack_group(needed)

        def advance(step, carry):
            target, needed = plan(step - 1)[0], plan(step)[1]
            await_group(needed, GROUP)
            bin_group(target)
            unpack_group(needed)
            return carry

        lax.fori_loop(1, GROUPS - 1, advance, 0)
        bin_group(plan(GROUPS - 2)[0])
        bin_group(plan(GROUPS - 1)[0])
        sums[...] = binned().reshape(BINS, 1, 2 * LANES)

    slot = band * CHUNKS + my_chunk

    @pl.when(gathers)
    def _():
        pl.run_scoped(correlate, *(unit((BINS, 2 * LANES), jnp.float32) for unit in units))
        gathered[slot] = sums[me]

        for there in range(N_FRQ):
            for y_low in range(2):
                for z_at in range(4):
                    base = z_at * 4 + y_low * 2

                    def deliver(step, carry, base=base, there=there):
                        to = step // 2 * 16 + base + step % 2

                        @pl.when(jnp.logical_or(to != me, there != band))
                        def _():
                            pltpu.make_async_remote_copy(
                                src_ref=sums.at[to],
                                dst_ref=gathered.at[slot],
                                send_sem=row_send_sem,
                                recv_sem=row_sem,
                                device_id=(to, there),
                                device_id_type=MESH,
                            ).start()

                        return carry

                    lax.fori_loop(0, 8, deliver, 0, unroll=True)

    for copy in table_copies:
        copy.wait()

    @pl.when(gathers)
    def _():
        await_all(send, CHUNKS - 1, send_sem)
        await_all(keys, CHUNKS - 1, key_send_sem)
        await_all(gathered, SLOTS - 1, row_send_sem)
        await_all(gathered, SLOTS, row_send_sem)

    @pl.when(jnp.logical_not(gathers))
    def _():
        await_all(send, CHUNKS, send_sem)
        await_all(keys, CHUNKS, key_send_sem)

    def finish(*accs):
        push_tables(high, low, accs)

        @pl.when(gathers)
        def _():
            await_all(gathered, SLOTS - 1, row_sem)

        @pl.when(jnp.logical_not(gathers))
        def _():
            await_all(gathered, SLOTS, row_sem)

        transform(gathered, fine, stack_ref, out_ref, accs)

    pl.run_scoped(finish, *(unit((LANES, 2 * LANES), jnp.float32) for unit in units))


def local(spectra, pair_bin, pair_valid, stack_in):
    high, low, fine = tables()
    block = (N_STN, STN, LANES)
    twin = (N_STN, 2 * STN, LANES)
    return pl.pallas_call(
        kernel,
        out_shape=jax.ShapeDtypeStruct((1, HALF), jnp.float32),
        in_specs=[pl.BlockSpec(memory_space=pltpu.HBM)] * 7,
        out_specs=pl.BlockSpec(memory_space=pltpu.VMEM),
        scratch_shapes=[
            pltpu.VMEM((STN, 2, BAND), jnp.bfloat16),
            pltpu.VMEM((ROWS, LANES), jnp.int32),
            pltpu.VMEM((ROWS, LANES), jnp.int32),
            pltpu.VMEM((1, HALF), jnp.float32),
            pltpu.VMEM((CHUNKS, 2 * STN, LANES), jnp.bfloat16),
            pltpu.VMEM(twin, jnp.bfloat16),
            pltpu.VMEM((ROWS, LANES), jnp.bfloat16),
            pltpu.VMEM((N_STN, ROWS, LANES), jnp.bfloat16),
            pltpu.VMEM((N_STN, ROWS, LANES), jnp.float32),
            pltpu.VMEM(block, jnp.float32),
            pltpu.VMEM(block, jnp.float32),
            pltpu.VMEM(twin, jnp.bfloat16),
            pltpu.VMEM(twin, jnp.bfloat16),
            pltpu.VMEM((BINS, 1, 2 * LANES), jnp.float32),
            pltpu.VMEM((SLOTS, 1, 2 * LANES), jnp.float32),
            pltpu.VMEM(high.shape, jnp.bfloat16),
            pltpu.VMEM(low.shape, jnp.bfloat16),
            pltpu.VMEM(fine.shape[1:], jnp.float32),
            pltpu.SemaphoreType.DMA,
            pltpu.SemaphoreType.DMA((6,)),
            pltpu.SemaphoreType.DMA,
            pltpu.SemaphoreType.DMA,
            pltpu.SemaphoreType.DMA((GROUPS,)),
            pltpu.SemaphoreType.DMA((GROUPS,)),
            pltpu.SemaphoreType.DMA,
            pltpu.SemaphoreType.DMA,
        ],
        compiler_params=pltpu.CompilerParams(
            collective_id=0, has_side_effects=True, vmem_limit_bytes=32 * 2**20
        ),
    )(
        *(
            pltpu.with_memory_space_constraint(operand, pltpu.HBM)
            for operand in (
                spectra,
                pair_bin.reshape(ROWS, LANES),
                pair_valid.reshape(ROWS, LANES),
                stack_in,
                jnp.asarray(high),
                jnp.asarray(low),
                jnp.asarray(fine),
            )
        )
    )


def solution(mesh):
    placed = (P("stn", None, "frq"), P("stn", None), P("stn"), P("stn", "frq"))
    return jax.shard_map(
        local, mesh=mesh, in_specs=placed, out_specs=P("stn", "frq"), check_vma=False
    )
```
